32 devices in a mesh: seq: 8 (over z, core), chan: 4 (over y, x).
Axes of the slice: x: 2, y: 2, z: 4, core: 2. Of those that a mesh axis runs over, the one named last changes fastest.
Arguments:
- query_proj: bfloat16 [1024, 8192], P('seq', 'chan'), may hold values from -6 to 6
- key_proj: bfloat16 [1024, 8192], P('seq', 'chan'), may hold values from -6 to 6
- value_proj: bfloat16 [1024, 8192], P('seq', 'chan'), may hold values from -6 to 6
- short_filter: float32 [3, 512, 3], P(None, 'chan'), may hold values from -2.4 to 2.4
- long_filter: bfloat16 [512, 1024], P('chan'), may hold values from -4 to 4
- out_weight: bfloat16 [8192, 8192], P(None, 'chan'), may hold values from -0.09375 to 0.09375
- grad_out: bfloat16 [1024, 8192], P('seq', 'chan'), may hold values from -6 to 6
Outputs:
- mixer_out: bfloat16 [1024, 8192], P('seq', 'chan')
- grad_query: bfloat16 [1024, 8192], P('seq', 'chan')
- grad_key: bfloat16 [1024, 8192], P('seq', 'chan')
- grad_value: bfloat16 [1024, 8192], P('seq', 'chan')
The draws below stay inside these ranges and needn't reach their ends.
All inputs are finite; a program needn't handle non-finite values.
Results may differ from the reference program's by a relative error of at most 0.0064.
Values may be sent and summed in bfloat16 or wider, within the bound.
A program may use at most 128 MiB of HBM per device.

```python
import math
import jax
import jax.numpy as jnp
from jax import lax

D = 8192
GROUP = 16
SHORT = 3
FILTER_GROUPS = 512
SEQUENCE_LENGTH = 1024


def draw_long_filter(key, part):
    key_rows = jax.random.split(key, 6)
    delay_offsets = jnp.arange(SEQUENCE_LENGTH, dtype=jnp.float32)[None, :]
    slow = jnp.exp(jax.random.uniform(key_rows[0], (FILTER_GROUPS, 1), minval=math.log(SEQUENCE_LENGTH), maxval=math.log(8.0 * SEQUENCE_LENGTH)))
    quick = jnp.exp(jax.random.uniform(key_rows[1], (FILTER_GROUPS, 1), minval=math.log(20.0), maxval=math.log(60.0)))
    picked = jax.random.uniform(key_rows[2], (FILTER_GROUPS, 1)) < 0.5
    noise = jnp.clip(jax.random.normal(key_rows[3], (FILTER_GROUPS, SEQUENCE_LENGTH)), -4.0, 4.0)
    scale = jnp.where(picked, quick, slow)
    decay_profile = jnp.exp(-delay_offsets / scale)
    spike_position = jax.random.randint(key_rows[4], (FILTER_GROUPS, 2), 1, SEQUENCE_LENGTH).astype(jnp.float32)
    spike_retained = jax.random.uniform(key_rows[5], (FILTER_GROUPS, 2), minval=0.5, maxval=0.8)
    decay_profile = decay_profile * jnp.where(delay_offsets >= spike_position[:, 0:1], spike_retained[:, 0:1], 1.0)
    decay_profile = decay_profile * jnp.where(delay_offsets >= spike_position[:, 1:2], spike_retained[:, 1:2], 1.0)
    energy = (1.0 - jnp.exp(-2.0 * SEQUENCE_LENGTH / scale)) / (1.0 - jnp.exp(-2.0 / scale))
    return (noise * decay_profile / jnp.sqrt(energy)).astype(jnp.bfloat16)


def raised(entries, stream_key, source, target, parts, factor):
    def block_of(position):
        return (jnp.arange(entries.shape[position]) // (entries.shape[position] // parts)).reshape((-1,) + (1,) * (entries.ndim - 1 - position))

    near = jax.random.permutation(stream_key, parts)[block_of(target)]
    other_side = (block_of(target) + parts // 2) % parts
    return jnp.where((block_of(source) == near) | (block_of(source) == other_side), factor * entries, entries)


def shard_levels(rng, shape, shards, least, high):
    def one(axis_at, shards_of):
        draws = jax.random.uniform(jax.random.fold_in(jax.random.fold_in(rng, 6), axis_at), (shards_of,), jnp.float32, least / len(shards), high / len(shards))
        return jnp.repeat(jnp.exp(draws), shape[axis_at] // shards_of).reshape((-1,) + (1,) * (len(shape) - axis_at - 1))

    level = one(*shards[0])
    for cut in shards[1:]:
        level = level * one(*cut)
    return level


def normal_values(key, shape, width, most, shards=(), kind=jnp.bfloat16):
    values = jax.random.normal(key, shape, jnp.float32) * width
    if len(shards) > 0:
        values = shard_levels(key, shape, shards, -0.22, 0.18) * values
    return jnp.clip(values, min=-most, max=most).astype(kind)


def bell_draw_with(rng, dims, spread, reach, pieces, heavy, held_as=jnp.bfloat16):
    drawn = spread * jax.random.normal(rng, dims, jnp.float32)
    if pieces:
        drawn = drawn * shard_levels(rng, dims, pieces, -0.22, 0.18)
    return jnp.clip(raised(drawn, jax.random.fold_in(rng, 3), *heavy), -reach, reach).astype(held_as)


def setup_inputs(seed: int = 0) -> dict:
    seeds = jax.random.split(jax.random.key(seed), 8)
    query_proj = normal_values(seeds[0], (SEQUENCE_LENGTH, D), 1.0, 6.0, ((0, 8), (1, 4)))
    key_proj = normal_values(seeds[1], (SEQUENCE_LENGTH, D), 1.0, 6.0, ((0, 8), (1, 4)))
    value_proj = normal_values(seeds[2], (SEQUENCE_LENGTH, D), 1.0, 6.0, ((0, 8), (1, 4)))
    short_filter = normal_values(seeds[3], (3, FILTER_GROUPS, SHORT), 0.4, 2.4, ((1, 4),), jnp.float32)
    long_filter = draw_long_filter(jax.random.fold_in(seeds[7], 71), 0)
    out_weight = bell_draw_with(seeds[5], (D, D), D ** -0.5, 0.09375, ((1, 4),), (1, 0, 4, 2.0))
    grad_out = normal_values(seeds[6], (SEQUENCE_LENGTH, D), 1.0, 6.0, ((0, 8), (1, 4)))
    return dict(query_proj=query_proj, key_proj=key_proj, value_proj=value_proj, short_filter=short_filter, long_filter=long_filter, out_weight=out_weight, grad_out=grad_out)


def widen_taps(taps):
    return jnp.repeat(taps, GROUP, axis=0)


def causal_taps(stream, taps):
    values = stream.astype(jnp.float32)
    per_chan = widen_taps(taps)
    total = jnp.zeros_like(values)
    for lag_index in range(SHORT):
        moved = jnp.concatenate([jnp.zeros((lag_index, D), values.dtype), values[:SEQUENCE_LENGTH - lag_index]], axis=0)
        total = total + moved * per_chan[:, lag_index]
    return total


def anticausal_taps(grads, taps):
    values = grads.astype(jnp.float32)
    per_chan = widen_taps(taps)
    total = jnp.zeros_like(values)
    for lag_index in range(SHORT):
        moved = jnp.concatenate([values[lag_index:], jnp.zeros((lag_index, D), values.dtype)], axis=0)
        total = total + moved * per_chan[:, lag_index]
    return total


def long_mix(values, filt):
    span = math.gcd(FILTER_GROUPS, 32)
    count = FILTER_GROUPS // span
    grouped = values.reshape(SEQUENCE_LENGTH, count, span, GROUP).transpose(1, 0, 2, 3)
    filt_blocks = filt.reshape(count, span, SEQUENCE_LENGTH)

    def mix_block(bundle):
        block_vals, block_filt = bundle
        spectrum = jnp.fft.rfft(block_vals, n=2 * SEQUENCE_LENGTH, axis=0)
        kernel = jnp.fft.rfft(block_filt.T, n=2 * SEQUENCE_LENGTH, axis=0)
        joined = jnp.fft.irfft(spectrum * kernel[:, :, None], n=2 * SEQUENCE_LENGTH, axis=0)
        return joined[:SEQUENCE_LENGTH]

    result = lax.map(mix_block, (grouped, filt_blocks))
    return result.transpose(1, 0, 2, 3).reshape(SEQUENCE_LENGTH, D)


def reference(query_proj, key_proj, value_proj, short_filter, long_filter, out_weight, grad_out):
    query_f = causal_taps(query_proj, short_filter[0])
    key_f = causal_taps(key_proj, short_filter[1])
    value_f = causal_taps(value_proj, short_filter[2])
    products = (key_f * value_f).astype(jnp.bfloat16)
    filt = long_filter.astype(jnp.float32)
    mixed = long_mix(products.astype(jnp.float32), filt).astype(jnp.bfloat16)
    mixed_f = mixed.astype(jnp.float32)
    gated = (query_f * mixed_f).astype(jnp.bfloat16)
    mixer_out = jnp.dot(gated, out_weight, preferred_element_type=jnp.float32).astype(jnp.bfloat16)
    grad_gated = jnp.dot(grad_out, out_weight.T, preferred_element_type=jnp.float32)
    grad_qf = (grad_gated * mixed_f).astype(jnp.bfloat16)
    grad_mixed = (grad_gated * query_f).astype(jnp.bfloat16)
    grad_prod = long_mix(grad_mixed.astype(jnp.float32)[::-1], filt)[::-1].astype(jnp.bfloat16)
    grad_pf = grad_prod.astype(jnp.float32)
    grad_kf = (grad_pf * value_f).astype(jnp.bfloat16)
    grad_vf = (grad_pf * key_f).astype(jnp.bfloat16)
    grad_query = anticausal_taps(grad_qf, short_filter[0]).astype(jnp.bfloat16)
    grad_key = anticausal_taps(grad_kf, short_filter[1]).astype(jnp.bfloat16)
    grad_value = anticausal_taps(grad_vf, short_filter[2]).astype(jnp.bfloat16)
    return (mixer_out, grad_query, grad_key, grad_value)
```

```python
import functools

import jax
import jax.numpy as jnp
from jax import lax
from jax.experimental import pallas as pl
from jax.experimental.pallas import tpu as pltpu
from jax.sharding import PartitionSpec as P

GROUP = 16
F32 = jnp.float32
BF16 = jnp.bfloat16


def passed_along(array, by):
    size = lax.axis_size("seq")
    pairs = [(i, i + by) for i in range(size) if 0 <= i + by < size]
    return lax.ppermute(array, "seq", pairs)


def causal(x, before, taps):
    row = lax.broadcasted_iota(jnp.int32, x.shape, 0)
    one = jnp.where(row == 0, before[1:2], pltpu.roll(x, 1, 0))
    two = jnp.where(row == 0, before[0:1], jnp.where(row == 1, before[1:2], pltpu.roll(x, 2, 0)))
    return x * taps[0:1] + one * taps[1:2] + two * taps[2:3]


def anticausal(g, after, taps):
    count = g.shape[0]
    row = lax.broadcasted_iota(jnp.int32, g.shape, 0)
    one = jnp.where(row == count - 1, after[0:1], pltpu.roll(g, count - 1, 0))
    two = jnp.where(
        row == count - 1,
        after[1:2],
        jnp.where(row == count - 2, after[0:1], pltpu.roll(g, count - 2, 0)),
    )
    return g * taps[0:1] + one * taps[1:2] + two * taps[2:3]


def products_kernel(k_ref, v_ref, before_ref, taps_ref, out_ref):
    before = before_ref[...].astype(F32)
    kf = causal(k_ref[...].astype(F32), before[2:4], taps_ref[3:6])
    vf = causal(v_ref[...].astype(F32), before[4:6], taps_ref[6:9])
    out_ref[...] = (kf * vf).T.astype(BF16)


def toeplitz_kernel(h_ref, hr_ref, fwd_ref, bwd_ref):
    groups, length = h_ref.shape
    block = fwd_ref.shape[2]
    for g in range(groups):
        pad = jnp.zeros((block, block), F32)
        rows = jnp.broadcast_to(h_ref[g : g + 1, :].astype(F32), (block, length))
        lined = pltpu.roll(
            jnp.concatenate([pad, rows], axis=1), 0, 1, stride=1, stride_axis=0
        ).astype(BF16)
        for k in range(length // block):
            fwd_ref[g, k * block : (k + 1) * block, :] = lined[:, (k + 1) * block : (k + 2) * block]
        rows = jnp.broadcast_to(hr_ref[g : g + 1, :].astype(F32), (block, length))
        lined = pltpu.roll(
            jnp.concatenate([rows, pad], axis=1), 1, 1, stride=1, stride_axis=0
        ).astype(BF16)
        for k in range(length // block):
            at = length - k * block
            bwd_ref[g, k * block : (k + 1) * block, :] = lined[:, at : at + block]


def mix_kernel(forward, x_ref, filt_ref, out_ref):
    blocks, groups, width, block = x_ref.shape
    rows = blocks * width
    for g in range(groups):
        x = x_ref[:, g]
        if width % 16:
            x = x.astype(F32)
        x = x.reshape(rows, block).astype(BF16)
        parts = [x]
        for k in range(1, blocks):
            pad = jnp.zeros((k * width, block), F32 if width % 16 else BF16)
            src = x.astype(pad.dtype)
            if forward:
                moved = jnp.concatenate([pad, src[: rows - k * width]], axis=0)
            else:
                moved = jnp.concatenate([src[k * width :], pad], axis=0)
            parts.append(moved.astype(BF16))
        total = jnp.dot(
            jnp.concatenate(parts, axis=1), filt_ref[g], preferred_element_type=F32
        )
        out_ref[:, g] = total.reshape(blocks, width, block).astype(BF16)


def gate_kernel(q_ref, before_ref, taps_ref, mixed_ref, out_ref):
    qf = causal(q_ref[...].astype(F32), before_ref[...].astype(F32)[0:2], taps_ref[0:3])
    out_ref[...] = (qf * mixed_ref[...].astype(F32).T).astype(BF16)


def grad_mixed_kernel(q_ref, before_ref, taps_ref, parts_ref, out_ref):
    qf = causal(q_ref[...].astype(F32), before_ref[...].astype(F32)[0:2], taps_ref[0:3])
    total = jnp.sum(parts_ref[...].astype(F32), axis=0)
    out_ref[...] = (total * qf.T).astype(BF16)


def grad_query_kernel(mixed_ref, parts_ref, out_ref):
    total = jnp.sum(parts_ref[...].astype(F32), axis=0)
    out_ref[...] = (total * mixed_ref[...].astype(F32)).T.astype(BF16)


def last_kernel(
    k_ref, v_ref, before_ref, after_ref, taps_ref, gqf_ref, gqf_next_ref, gp_ref, gp_next_ref,
    gq_ref, gk_ref, gv_ref,
):
    count = k_ref.shape[0]
    before = before_ref[...].astype(F32)
    after = after_ref[...].astype(F32)
    gqf_next = gqf_next_ref[...].astype(F32)
    gp_next = gp_next_ref[...].astype(F32)

    def rounded(x):
        return x.astype(BF16).astype(F32)

    def filtered(ref, at):
        x = ref[...].astype(F32)
        taps = taps_ref[3 * at : 3 * at + 3]
        new = after[2 * at - 2 : 2 * at]
        f = causal(x, before[2 * at : 2 * at + 2], taps)
        last, ahead = x[count - 1 : count], x[count - 2 : count - 1]
        first = new[0:1] * taps[0:1] + last * taps[1:2] + ahead * taps[2:3]
        second = new[1:2] * taps[0:1] + new[0:1] * taps[1:2] + last * taps[2:3]
        return f, jnp.concatenate([first, second], axis=0)

    kf, kf_next = filtered(k_ref, 1)
    vf, vf_next = filtered(v_ref, 2)
    gp = gp_ref[...].astype(F32).T
    gq_ref[...] = anticausal(gqf_ref[...].astype(F32), gqf_next, taps_ref[0:3]).astype(BF16)
    gk_ref[...] = anticausal(
        rounded(gp * vf), rounded(gp_next * vf_next), taps_ref[3:6]
    ).astype(BF16)
    gv_ref[...] = anticausal(
        rounded(gp * kf), rounded(gp_next * kf_next), taps_ref[6:9]
    ).astype(BF16)


def params(mib=48):
    return pltpu.CompilerParams(vmem_limit_bytes=mib * 1024 * 1024)


def cost(flops, nbytes):
    return pl.CostEstimate(flops=flops, bytes_accessed=nbytes, transcendentals=0)


def local(query_proj, key_proj, value_proj, short_filter, long_filter, out_weight, grad_out):
    count, width = query_proj.shape
    seq = lax.axis_size("seq")
    chan = lax.axis_size("chan")
    per = width // seq
    gw = min(per, GROUP)
    groups = per // gw
    length = long_filter.shape[1]
    tile = min(512, width)
    steps = width // tile

    taps = jnp.repeat(short_filter.transpose(0, 2, 1).reshape(9, -1), GROUP, axis=1)
    before = passed_along(
        jnp.concatenate([a[count - 2 :] for a in (query_proj, key_proj, value_proj)], axis=0), 1
    )
    after = passed_along(jnp.concatenate([a[:2] for a in (key_proj, value_proj)], axis=0), -1)
    first = lax.axis_index("seq") * per // GROUP
    chosen = lax.dynamic_slice_in_dim(long_filter, first, groups, 0)

    def tall(rows):
        return pl.BlockSpec((rows, tile), lambda i: (0, i))

    wide = pl.BlockSpec((tile, count), lambda i: (i, 0))
    stacked = pl.BlockSpec((chan, tile, count), lambda i: (0, i, 0))
    flat = jax.ShapeDtypeStruct((count, width), BF16)
    turned = jax.ShapeDtypeStruct((width, count), BF16)
    size = 2 * count * width

    parts = lax.dot_general(
        out_weight, grad_out, (((1,), (1,)), ((), ())), preferred_element_type=F32
    ).astype(BF16)
    parts = lax.all_to_all(parts.reshape(chan, width, count), "chan", 0, 0)

    products = pl.pallas_call(
        products_kernel,
        grid=(steps,),
        in_specs=[tall(count), tall(count), tall(6), tall(9)],
        out_specs=wide,
        out_shape=turned,
        compiler_params=params(),
        cost_estimate=cost(12 * count * width, 3 * size),
        name="products",
    )(key_proj, value_proj, before, taps)

    some = min(groups, 4)
    fwd_filt, bwd_filt = pl.pallas_call(
        toeplitz_kernel,
        grid=(max(1, groups // 8),),
        in_specs=[pl.BlockSpec((min(8, groups), length), lambda i: (i, 0))] * 2,
        out_specs=[pl.BlockSpec((min(8, groups), length, count), lambda i: (i, 0, 0))] * 2,
        out_shape=[jax.ShapeDtypeStruct((groups, length, count), BF16)] * 2,
        compiler_params=params(),
        cost_estimate=cost(20 * groups * length * count, 4 * groups * length * count),
        name="toeplitz",
    )(chosen, chosen[:, ::-1])

    def mix(values, filt, forward):
        values = lax.all_to_all(values.reshape(seq, per, count), "seq", 0, 0)
        spec = pl.BlockSpec((seq, some, gw, count), lambda i: (0, i, 0, 0))
        out = pl.pallas_call(
            functools.partial(mix_kernel, forward),
            grid=(groups // some,),
            in_specs=[spec, pl.BlockSpec((some, length, count), lambda i: (i, 0, 0))],
            out_specs=spec,
            out_shape=jax.ShapeDtypeStruct((seq, groups, gw, count), BF16),
            compiler_params=params(),
            cost_estimate=cost(
                2 * groups * seq * gw * length * count, 2 * size + 2 * groups * length * count
            ),
            name="mix",
        )(values.reshape(seq, groups, gw, count), filt)
        return lax.all_to_all(out.reshape(seq, per, count), "seq", 0, 0).reshape(width, count)

    mixed = mix(products, fwd_filt, True)

    grad_mixed = pl.pallas_call(
        grad_mixed_kernel,
        grid=(steps,),
        in_specs=[tall(count), tall(6), tall(9), stacked],
        out_specs=wide,
        out_shape=turned,
        compiler_params=params(),
        cost_estimate=cost(12 * count * width, (2 + chan) * size),
        name="grad_mixed",
    )(query_proj, before, taps, parts)
    grad_prod = mix(grad_mixed, bwd_filt, False)

    gated = pl.pallas_call(
        gate_kernel,
        grid=(steps,),
        in_specs=[tall(count), tall(6), tall(9), wide],
        out_specs=tall(count),
        out_shape=flat,
        compiler_params=params(),
        cost_estimate=cost(8 * count * width, 3 * size),
        name="gate",
    )(query_proj, before, taps, mixed)
    mixer_out = jnp.dot(
        lax.all_gather(gated, "chan", axis=1, tiled=True),
        out_weight,
        preferred_element_type=F32,
    ).astype(BF16)

    grad_qf = pl.pallas_call(
        grad_query_kernel,
        grid=(steps,),
        in_specs=[wide, stacked],
        out_specs=tall(count),
        out_shape=flat,
        compiler_params=params(),
        cost_estimate=cost(8 * count * width, (2 + chan) * size),
        name="grad_query",
    )(mixed, parts)
    grad_qf_next = passed_along(grad_qf[:2], -1)
    grad_prod_next = passed_along(grad_prod[:, :2].T, -1)

    grads = pl.pallas_call(
        last_kernel,
        grid=(steps,),
        in_specs=[
            tall(count), tall(count), tall(6), tall(4), tall(9), tall(count), tall(2), wide, tall(2),
        ],
        out_specs=[tall(count)] * 3,
        out_shape=[flat] * 3,
        compiler_params=params(),
        cost_estimate=cost(40 * count * width, 7 * size),
        name="last",
    )(
        key_proj, value_proj, before, after, taps, grad_qf, grad_qf_next, grad_prod, grad_prod_next
    )
    return (mixer_out, *grads)


def solution(mesh):
    return jax.shard_map(
        local,
        mesh=mesh,
        in_specs=(
            P("seq", "chan"),
            P("seq", "chan"),
            P("seq", "chan"),
            P(None, "chan", None),
            P("chan", None),
            P(None, "chan"),
            P("seq", "chan"),
        ),
        out_specs=(P("seq", "chan"), P("seq", "chan"), P("seq", "chan"), P("seq", "chan")),
        check_vma=False,
    )
```

```python
import jax
import jax.numpy as jnp
from jax import lax
from jax.experimental import pallas as pl
from jax.experimental.pallas import tpu as pltpu
from jax.sharding import PartitionSpec as P

GROUP = 16
F32 = jnp.float32
BF16 = jnp.bfloat16
MESH = pl.DeviceIdType.MESH


def causal(x, before, taps):
    row = lax.broadcasted_iota(jnp.int32, x.shape, 0)
    one = jnp.where(row == 0, before[1:2], pltpu.roll(x, 1, 0))
    two = jnp.where(row == 0, before[0:1], jnp.where(row == 1, before[1:2], pltpu.roll(x, 2, 0)))
    return x * taps[0:1] + one * taps[1:2] + two * taps[2:3]


def anticausal(g, after, taps):
    count = g.shape[0]
    row = lax.broadcasted_iota(jnp.int32, g.shape, 0)
    one = jnp.where(row == count - 1, after[0:1], pltpu.roll(g, count - 1, 0))
    two = jnp.where(
        row == count - 1,
        after[1:2],
        jnp.where(row == count - 2, after[0:1], pltpu.roll(g, count - 2, 0)),
    )
    return g * taps[0:1] + one * taps[1:2] + two * taps[2:3]


def rounded(x):
    return x.astype(BF16).astype(F32)


def step_kernel(
    q_ref, k_ref, v_ref, taps_ref, h_ref, hr_ref, w_hbm, go_ref,
    out_ref, gq_ref, gk_ref, gv_ref,
    w_ref, got_ref, filt_ref, send_refs, recv_refs, part_send, part_recv, gall_ref, acc_ref,
    gqf_ref, gp_ref, hsend_ref, hrecv_ref, tail_ref, head_ref,
    w_sem, seq_send, seq_recv, chan_send, chan_recv, halo_send, halo_recv,
):
    seq = lax.axis_size("seq")
    chan = lax.axis_size("chan")
    here = lax.axis_index("seq")
    mine = lax.axis_index("chan")
    count, width = q_ref.shape
    _, groups, gw, _ = recv_refs.shape[1:]
    per = groups * gw
    length = h_ref.shape[1]
    columns = go_ref.shape[1]
    tile = max(per, min(256, width))
    tiles = width // tile
    dests = tile // per
    rows = min(512, width)
    wide = min(512, columns)

    def seq_peer(off):
        return lax.rem(here + off, seq)

    def chan_peer(off):
        return lax.rem(mine + off, chan)

    def w_copy(off):
        at = pl.ds(pl.multiple_of(chan_peer(off) * width, width), width)
        return pltpu.make_async_copy(w_hbm.at[at], w_ref.at[at], w_sem.at[off])

    order = [off % chan for off in range(1, chan + 1)]
    for off in order:
        w_copy(off).start()

    barrier = pltpu.get_barrier_semaphore()

    def greet_seq(off, carry):
        pl.semaphore_signal(
            barrier, inc=1, device_id={"seq": seq_peer(off)}, device_id_type=MESH
        )
        return carry

    def greet_chan(off, carry):
        pl.semaphore_signal(
            barrier, inc=1, device_id={"chan": chan_peer(off)}, device_id_type=MESH
        )
        return carry

    lax.fori_loop(1, seq, greet_seq, 0)
    lax.fori_loop(1, chan, greet_chan, 0)

    for m, ref in enumerate((q_ref, k_ref, v_ref)):
        hsend_ref[0, 2 * m : 2 * m + 2, :] = ref[count - 16 :, :].astype(F32)[14:]
        hsend_ref[1, 2 * m : 2 * m + 2, :] = ref[:16, :].astype(F32)[:2]
    pl.semaphore_wait(barrier, seq + chan - 2)

    def halo(slot, by, src, dst):
        return pltpu.make_async_remote_copy(
            src_ref=src, dst_ref=dst, send_sem=halo_send.at[slot], recv_sem=halo_recv.at[slot],
            device_id={"seq": seq_peer(by)}, device_id_type=MESH,
        )

    halo_down = halo(0, 1, hsend_ref.at[0, 0:6], hrecv_ref.at[0, 0:6])
    halo_up = halo(1, seq - 1, hsend_ref.at[1, 0:6], hrecv_ref.at[1, 0:6])
    halo_down.start()
    halo_up.start()

    def turn(i, carry):
        at = pl.ds(pl.multiple_of(i * wide, wide), wide)
        got_ref[at, :] = go_ref[:, at].astype(F32).T.astype(BF16)
        return carry

    lax.fori_loop(0, columns // wide, turn, 0)

    def exchange(slot, off):
        return pltpu.make_async_remote_copy(
            src_ref=send_refs.at[slot, seq_peer(off)],
            dst_ref=recv_refs.at[slot, here],
            send_sem=seq_send.at[slot, off],
            recv_sem=seq_recv.at[slot, off],
            device_id={"seq": seq_peer(off)},
            device_id_type=MESH,
        )

    def exchange_start(slot):
        def go(off, carry):
            exchange(slot, off).start()
            return carry

        lax.fori_loop(1, seq, go, 0)
        recv_refs[slot, pl.ds(here, 1)] = send_refs[slot, pl.ds(here, 1)]

    def exchange_wait(slot):
        def go(off, carry):
            exchange(slot, off).wait()
            return carry

        lax.fori_loop(1, seq, go, 0)

    def to_send(slot, i, turned):
        send_refs[slot, pl.ds(i * dests, dests)] = turned.reshape(
            dests, groups, gw, count
        ).astype(BF16)

    def from_recv(slot, i):
        return recv_refs[slot, pl.ds(i * dests, dests)].astype(F32).reshape(tile, count)

    def cols(i):
        return pl.ds(pl.multiple_of(i * tile, tile), tile)

    def filtered(ref, m, at):
        ahead = jnp.where(here > 0, hrecv_ref[0, 2 * m : 2 * m + 2, at], 0.0)
        return causal(ref[:, at].astype(F32), ahead, taps_ref[3 * m : 3 * m + 3, at])

    halo_down.wait()
    halo_up.wait()

    def products(i, carry):
        at = cols(i)
        to_send(0, i, (filtered(k_ref, 1, at) * filtered(v_ref, 2, at)).T)
        return carry

    lax.fori_loop(0, tiles, products, 0)
    exchange_start(0)

    def part(off):
        return pltpu.make_async_remote_copy(
            src_ref=part_send.at[off - 1],
            dst_ref=part_recv.at[mine],
            send_sem=chan_send.at[0, off],
            recv_sem=chan_recv.at[0, off],
            device_id={"chan": chan_peer(off)},
            device_id_type=MESH,
        )

    for off in order:
        w_copy(off).wait()

        def some(i, carry, off=off):
            start = pl.multiple_of(chan_peer(off) * width + i * rows, rows)
            got = jnp.dot(w_ref[pl.ds(start, rows), :], got_ref[...], preferred_element_type=F32)
            at = pl.ds(pl.multiple_of(i * rows, rows), rows)
            if off:
                part_send[off - 1, at, :] = got.astype(BF16)
            else:
                part_recv[mine, at, :] = got.astype(BF16)
            return carry

        lax.fori_loop(0, width // rows, some, 0)
        if off:
            part(off).start()

    def build(forward):
        def one(g, carry):
            pad = jnp.zeros((count, count), F32)
            row = (h_ref if forward else hr_ref)[pl.ds(g, 1), :]
            lines = jnp.broadcast_to(row, (count, length))
            pair = [pad, lines] if forward else [lines, pad]
            lined = pltpu.roll(
                jnp.concatenate(pair, axis=1), 0 if forward else 1, 1, stride=1, stride_axis=0
            ).astype(BF16)
            for k in range(length // count):
                at = (k + 1) * count if forward else length - k * count
                filt_ref[g, k * count : (k + 1) * count, :] = lined[:, at : at + count]
            return carry

        lax.fori_loop(0, groups, one, 0)

    def mix(forward, slot):
        total_rows = seq * gw

        def one(g, carry):
            x = recv_refs[slot, :, g]
            kind = F32 if gw % 16 else BF16
            x = x.astype(kind).reshape(total_rows, count)
            pieces = [x.astype(BF16)]
            for k in range(1, seq):
                pad = jnp.zeros((k * gw, count), kind)
                if forward:
                    moved = jnp.concatenate([pad, x[: total_rows - k * gw]], axis=0)
                else:
                    moved = jnp.concatenate([x[k * gw :], pad], axis=0)
                pieces.append(moved.astype(BF16))
            total = jnp.dot(
                jnp.concatenate(pieces, axis=1), filt_ref[g], preferred_element_type=F32
            )
            send_refs[slot + 1, :, g] = total.reshape(seq, gw, count).astype(BF16)
            return carry

        lax.fori_loop(0, groups, one, 0)

    build(True)
    exchange_wait(0)
    mix(True, 0)
    exchange_start(1)
    build(False)

    for off in range(1, chan):
        part(off).wait()

    def summed(at):
        return jnp.sum(part_recv[:, at, :].astype(F32), axis=0)

    def grad_mixed(i, carry):
        at = cols(i)
        to_send(2, i, summed(at) * filtered(q_ref, 0, at).T)
        return carry

    lax.fori_loop(0, tiles, grad_mixed, 0)
    exchange_start(2)

    def share(off):
        return pltpu.make_async_remote_copy(
            src_ref=gall_ref.at[mine],
            dst_ref=gall_ref.at[mine],
            send_sem=chan_send.at[1, off],
            recv_sem=chan_recv.at[1, off],
            device_id={"chan": chan_peer(off)},
            device_id_type=MESH,
        )

    exchange_wait(1)

    def gate(i, carry):
        at = cols(i)
        gall_ref[mine, :, at] = (filtered(q_ref, 0, at) * from_recv(1, i).T).astype(BF16)
        return carry

    lax.fori_loop(0, tiles, gate, 0)
    for off in range(1, chan):
        share(off).start()

    def grad_query(i, carry):
        at = cols(i)
        gqf_ref[:, at] = rounded((summed(at) * from_recv(1, i)).T)
        return carry

    lax.fori_loop(0, tiles, grad_query, 0)

    def project(off, first, last):
        owner = chan_peer(chan - off)

        def some(i, carry):
            at = pl.ds(pl.multiple_of(i * wide, wide), wide)
            start = pl.multiple_of(owner * width, width)
            got = jnp.dot(
                gall_ref[owner], w_ref[pl.ds(start, width), at], preferred_element_type=F32
            )
            if not first:
                got = got + acc_ref[:, at]
            if last:
                out_ref[:, at] = got.astype(BF16)
            else:
                acc_ref[:, at] = got
            return carry

        lax.fori_loop(0, columns // wide, some, 0)

    project(0, True, chan == 1)
    exchange_wait(2)
    mix(False, 2)
    exchange_start(3)
    for off in range(1, chan):
        share(off).wait()
        project(off, False, off == chan - 1)

    exchange_wait(3)

    def grad_products(i, carry):
        at = cols(i)
        gp_ref[:, at] = from_recv(3, i).T
        return carry

    lax.fori_loop(0, tiles, grad_products, 0)
    tail_ref[0:2, :] = gqf_ref[0:2, :]
    tail_ref[2:4, :] = gp_ref[0:2, :]
    tail = halo(2, seq - 1, tail_ref, head_ref)
    tail.start()
    tail.wait()

    def last(i, carry):
        at = cols(i)

        def behind(ref, m):
            x = ref[count - 16 :, at].astype(F32)
            taps = taps_ref[3 * m : 3 * m + 3, at]
            new = hrecv_ref[1, 2 * m : 2 * m + 2, at]
            first = new[0:1] * taps[0:1] + x[15:16] * taps[1:2] + x[14:15] * taps[2:3]
            second = new[1:2] * taps[0:1] + new[0:1] * taps[1:2] + x[15:16] * taps[2:3]
            return jnp.concatenate([first, second], axis=0)

        def masked(rows_after):
            return jnp.where(here < seq - 1, rows_after, 0.0)

        gp = gp_ref[:, at]
        gp_next = head_ref[2:4, at]
        gq_ref[:, at] = anticausal(
            gqf_ref[:, at], masked(head_ref[0:2, at]), taps_ref[0:3, at]
        ).astype(BF16)
        gk_ref[:, at] = anticausal(
            rounded(gp * filtered(v_ref, 2, at)),
            masked(rounded(gp_next * behind(v_ref, 2))),
            taps_ref[3:6, at],
        ).astype(BF16)
        gv_ref[:, at] = anticausal(
            rounded(gp * filtered(k_ref, 1, at)),
            masked(rounded(gp_next * behind(k_ref, 1))),
            taps_ref[6:9, at],
        ).astype(BF16)
        return carry

    lax.fori_loop(0, tiles, last, 0)


def local(query_proj, key_proj, value_proj, short_filter, long_filter, out_weight, grad_out):
    count, width = query_proj.shape
    seq = lax.axis_size("seq")
    chan = lax.axis_size("chan")
    per = width // seq
    gw = min(per, GROUP)
    groups = per // gw
    length = long_filter.shape[1]
    depth, columns = out_weight.shape

    taps = jnp.repeat(short_filter.transpose(0, 2, 1).reshape(9, -1), GROUP, axis=1)
    first = lax.axis_index("seq") * per // GROUP
    chosen = lax.dynamic_slice_in_dim(long_filter, first, groups, 0).astype(F32)

    vmem = pl.BlockSpec(memory_space=pltpu.VMEM)
    flat = jax.ShapeDtypeStruct((count, width), BF16)
    return pl.pallas_call(
        step_kernel,
        in_specs=[vmem] * 6 + [pl.BlockSpec(memory_space=pl.ANY), vmem],
        out_specs=[vmem] * 4,
        out_shape=[jax.ShapeDtypeStruct((count, columns), BF16), flat, flat, flat],
        scratch_shapes=[
            pltpu.VMEM((depth, columns), BF16),
            pltpu.VMEM((columns, count), BF16),
            pltpu.VMEM((groups, length, count), BF16),
            pltpu.VMEM((4, seq, groups, gw, count), BF16),
            pltpu.VMEM((4, seq, groups, gw, count), BF16),
            pltpu.VMEM((chan - 1, width, count), BF16),
            pltpu.VMEM((chan, width, count), BF16),
            pltpu.VMEM((chan, count, width), BF16),
            pltpu.VMEM((count, columns), F32),
            pltpu.VMEM((count, width), F32),
            pltpu.VMEM((count, width), F32),
            pltpu.VMEM((2, 8, width), F32),
            pltpu.VMEM((2, 8, width), F32),
            pltpu.VMEM((4, width), F32),
            pltpu.VMEM((4, width), F32),
            pltpu.SemaphoreType.DMA((chan,)),
            pltpu.SemaphoreType.DMA((4, seq)),
            pltpu.SemaphoreType.DMA((4, seq)),
            pltpu.SemaphoreType.DMA((2, chan)),
            pltpu.SemaphoreType.DMA((2, chan)),
            pltpu.SemaphoreType.DMA((3,)),
            pltpu.SemaphoreType.DMA((3,)),
        ],
        compiler_params=pltpu.CompilerParams(
            collective_id=0, has_side_effects=True, vmem_limit_bytes=62 * 1024 * 1024
        ),
        name="step",
    )(query_proj, key_proj, value_proj, taps, chosen, chosen[:, ::-1], out_weight, grad_out)


def solution(mesh):
    return jax.shard_map(
        local,
        mesh=mesh,
        in_specs=(
            P("seq", "chan"),
            P("seq", "chan"),
            P("seq", "chan"),
            P(None, "chan", None),
            P("chan", None),
            P(None, "chan"),
            P("seq", "chan"),
        ),
        out_specs=(P("seq", "chan"), P("seq", "chan"), P("seq", "chan"), P("seq", "chan")),
        check_vma=False,
    )
```

```python
import jax
import jax.numpy as jnp
from jax import lax
from jax.experimental import pallas as pl
from jax.experimental.pallas import tpu as pltpu
from jax.sharding import PartitionSpec as P

GROUP = 16
F32 = jnp.float32
BF16 = jnp.bfloat16
MESH = pl.DeviceIdType.MESH


def causal(x, before, taps):
    row = lax.broadcasted_iota(jnp.int32, x.shape, 0)
    one = jnp.where(row == 0, before[1:2], pltpu.roll(x, 1, 0))
    two = jnp.where(row == 0, before[0:1], jnp.where(row == 1, before[1:2], pltpu.roll(x, 2, 0)))
    return x * taps[0:1] + one * taps[1:2] + two * taps[2:3]


def anticausal(g, after, taps):
    count = g.shape[0]
    row = lax.broadcasted_iota(jnp.int32, g.shape, 0)
    one = jnp.where(row == count - 1, after[0:1], pltpu.roll(g, count - 1, 0))
    two = jnp.where(
        row == count - 1,
        after[1:2],
        jnp.where(row == count - 2, after[0:1], pltpu.roll(g, count - 2, 0)),
    )
    return g * taps[0:1] + one * taps[1:2] + two * taps[2:3]


def rounded(x):
    return x.astype(BF16).astype(F32)


def step_kernel(
    q_ref, k_ref, v_ref, taps_ref, h_ref, w_hbm, go_ref,
    out_ref, gqf_ref, gp_ref, before_ref, after_ref,
    w_ref, got_ref, hr_ref, filt_ref, send_refs, recv_refs, part_send, part_recv, gall_ref,
    acc_ref, hsend_ref, hrecv_ref, tail_ref, head_ref,
    w_sem, seq_send, seq_recv, chan_send, chan_recv, halo_send, halo_recv,
):
    seq = lax.axis_size("seq")
    chan = lax.axis_size("chan")
    here = lax.axis_index("seq")
    mine = lax.axis_index("chan")
    count, width = q_ref.shape
    _, groups, gw, _ = recv_refs.shape[1:]
    per = groups * gw
    length = h_ref.shape[1]
    columns = go_ref.shape[1]
    tile = max(per, min(256, width))
    tiles = width // tile
    dests = tile // per
    rows = min(512, width)
    wide = min(512, columns)

    def seq_peer(off):
        return lax.rem(here + off, seq)

    def chan_peer(off):
        return lax.rem(mine + off, chan)

    def w_copy(off):
        at = pl.ds(pl.multiple_of(chan_peer(off) * width, width), width)
        return pltpu.make_async_copy(w_hbm.at[at], w_ref.at[at], w_sem.at[off])

    order = [off % chan for off in range(1, chan + 1)]
    for off in order:
        w_copy(off).start()

    barrier = pltpu.get_barrier_semaphore()

    def greet_seq(off, carry):
        pl.semaphore_signal(
            barrier, inc=1, device_id={"seq": seq_peer(off)}, device_id_type=MESH
        )
        return carry

    def greet_chan(off, carry):
        pl.semaphore_signal(
            barrier, inc=1, device_id={"chan": chan_peer(off)}, device_id_type=MESH
        )
        return carry

    lax.fori_loop(1, seq, greet_seq, 0)
    lax.fori_loop(1, chan, greet_chan, 0)

    for m, ref in enumerate((q_ref, k_ref, v_ref)):
        hsend_ref[0, 2 * m : 2 * m + 2, :] = ref[count - 16 :, :].astype(F32)[14:]
        hsend_ref[1, 2 * m : 2 * m + 2, :] = ref[:16, :].astype(F32)[:2]
    pl.semaphore_wait(barrier, seq + chan - 2)

    def halo(slot, by, src, dst):
        return pltpu.make_async_remote_copy(
            src_ref=src, dst_ref=dst, send_sem=halo_send.at[slot], recv_sem=halo_recv.at[slot],
            device_id={"seq": seq_peer(by)}, device_id_type=MESH,
        )

    halo_down = halo(0, 1, hsend_ref.at[0, 0:6], hrecv_ref.at[0, 0:6])
    halo_up = halo(1, seq - 1, hsend_ref.at[1, 0:6], hrecv_ref.at[1, 0:6])
    halo_down.start()
    halo_up.start()

    def turn(i, carry):
        at = pl.ds(pl.multiple_of(i * wide, wide), wide)
        got_ref[at, :] = go_ref[:, at].astype(F32).T.astype(BF16)
        return carry

    lax.fori_loop(0, columns // wide, turn, 0)

    def exchange(slot, off):
        return pltpu.make_async_remote_copy(
            src_ref=send_refs.at[slot, seq_peer(off)],
            dst_ref=recv_refs.at[slot, here],
            send_sem=seq_send.at[slot, off],
            recv_sem=seq_recv.at[slot, off],
            device_id={"seq": seq_peer(off)},
            device_id_type=MESH,
        )

    def exchange_start(slot):
        def go(off, carry):
            exchange(slot, off).start()
            return carry

        lax.fori_loop(1, seq, go, 0)
        recv_refs[slot, pl.ds(here, 1)] = send_refs[slot, pl.ds(here, 1)]

    def exchange_wait(slot):
        def go(off, carry):
            exchange(slot, off).wait()
            return carry

        lax.fori_loop(1, seq, go, 0)

    def to_send(slot, i, turned):
        send_refs[slot, pl.ds(i * dests, dests)] = turned.reshape(
            dests, groups, gw, count
        ).astype(BF16)

    def from_recv(slot, i):
        return recv_refs[slot, pl.ds(i * dests, dests)].astype(F32).reshape(tile, count)

    def cols(i):
        return pl.ds(pl.multiple_of(i * tile, tile), tile)

    def filtered(ref, m, at):
        ahead = jnp.where(here > 0, hrecv_ref[0, 2 * m : 2 * m + 2, at], 0.0)
        return causal(ref[:, at].astype(F32), ahead, taps_ref[3 * m : 3 * m + 3, at])

    halo_down.wait()
    halo_up.wait()

    def products(i, carry):
        at = cols(i)
        to_send(0, i, (filtered(k_ref, 1, at) * filtered(v_ref, 2, at)).T)
        return carry

    lax.fori_loop(0, tiles, products, 0)
    exchange_start(0)

    def part(off):
        return pltpu.make_async_remote_copy(
            src_ref=part_send.at[off - 1],
            dst_ref=part_recv.at[mine],
            send_sem=chan_send.at[0, off],
            recv_sem=chan_recv.at[0, off],
            device_id={"chan": chan_peer(off)},
            device_id_type=MESH,
        )

    def back_project(off):
        w_copy(off).wait()

        def some(i, carry):
            start = pl.multiple_of(chan_peer(off) * width + i * rows, rows)
            got = jnp.dot(w_ref[pl.ds(start, rows), :], got_ref[...], preferred_element_type=F32)
            at = pl.ds(pl.multiple_of(i * rows, rows), rows)
            if off:
                part_send[off - 1, at, :] = got.astype(BF16)
            else:
                part_recv[mine, at, :] = got.astype(BF16)
            return carry

        lax.fori_loop(0, width // rows, some, 0)
        if off:
            part(off).start()

    for off in range(1, chan):
        back_project(off)

    flip = (
        lax.broadcasted_iota(jnp.int32, (count, count), 0)
        + lax.broadcasted_iota(jnp.int32, (count, count), 1)
        == count - 1
    )
    flip = jnp.where(flip, 1.0, 0.0).astype(BF16)
    for k in range(length // count):
        hr_ref[:, length - (k + 1) * count : length - k * count] = jnp.dot(
            h_ref[:, k * count : (k + 1) * count].astype(BF16), flip, preferred_element_type=F32
        )

    def build(forward):
        def one(g, carry):
            pad = jnp.zeros((count, count), F32)
            row = (h_ref if forward else hr_ref)[pl.ds(g, 1), :]
            lines = jnp.broadcast_to(row, (count, length))
            pair = [pad, lines] if forward else [lines, pad]
            lined = pltpu.roll(
                jnp.concatenate(pair, axis=1), 0 if forward else 1, 1, stride=1, stride_axis=0
            ).astype(BF16)
            for k in range(length // count):
                at = (k + 1) * count if forward else length - k * count
                filt_ref[g, k * count : (k + 1) * count, :] = lined[:, at : at + count]
            return carry

        lax.fori_loop(0, groups, one, 0)

    def mix(forward, slot):
        total_rows = seq * gw

        def one(g, carry):
            x = recv_refs[slot, :, g]
            kind = F32 if gw % 16 else BF16
            x = x.astype(kind).reshape(total_rows, count)
            pieces = [x.astype(BF16)]
            for k in range(1, seq):
                pad = jnp.zeros((k * gw, count), kind)
                if forward:
                    moved = jnp.concatenate([pad, x[: total_rows - k * gw]], axis=0)
                else:
                    moved = jnp.concatenate([x[k * gw :], pad], axis=0)
                pieces.append(moved.astype(BF16))
            total = jnp.dot(
                jnp.concatenate(pieces, axis=1), filt_ref[g], preferred_element_type=F32
            )
            send_refs[slot + 1, :, g] = total.reshape(seq, gw, count).astype(BF16)
            return carry

        lax.fori_loop(0, groups, one, 0)

    build(True)
    exchange_wait(0)
    mix(True, 0)
    exchange_start(1)
    back_project(0)
    build(False)

    for off in range(1, chan):
        part(off).wait()

    def summed(at):
        return jnp.sum(part_recv[:, at, :].astype(F32), axis=0)

    def grad_mixed(i, carry):
        at = cols(i)
        to_send(2, i, summed(at) * filtered(q_ref, 0, at).T)
        return carry

    lax.fori_loop(0, tiles, grad_mixed, 0)
    exchange_start(2)

    def share(off):
        return pltpu.make_async_remote_copy(
            src_ref=gall_ref.at[mine],
            dst_ref=gall_ref.at[mine],
            send_sem=chan_send.at[1, off],
            recv_sem=chan_recv.at[1, off],
            device_id={"chan": chan_peer(off)},
            device_id_type=MESH,
        )

    exchange_wait(1)

    def gate(i, carry):
        at = cols(i)
        gall_ref[mine, :, at] = (filtered(q_ref, 0, at) * from_recv(1, i).T).astype(BF16)
        return carry

    lax.fori_loop(0, tiles, gate, 0)
    for off in range(1, chan):
        share(off).start()

    def grad_query(i, carry):
        at = cols(i)
        gqf_ref[:, at] = (summed(at) * from_recv(1, i)).T.astype(BF16)
        return carry

    lax.fori_loop(0, tiles, grad_query, 0)

    def project(off, first, last):
        owner = chan_peer(chan - off)

        def some(i, carry):
            at = pl.ds(pl.multiple_of(i * wide, wide), wide)
            start = pl.multiple_of(owner * width, width)
            got = jnp.dot(
                gall_ref[owner], w_ref[pl.ds(start, width), at], preferred_element_type=F32
            )
            if not first:
                got = got + acc_ref[:, at]
            if last:
                out_ref[:, at] = got.astype(BF16)
            else:
                acc_ref[:, at] = got
            return carry

        lax.fori_loop(0, columns // wide, some, 0)

    project(0, True, chan == 1)
    exchange_wait(2)
    mix(False, 2)
    exchange_start(3)
    for off in range(1, chan):
        share(off).wait()
        project(off, False, off == chan - 1)

    exchange_wait(3)

    def grad_products(i, carry):
        at = cols(i)
        gp_ref[:, at] = from_recv(3, i).T.astype(BF16)
        return carry

    lax.fori_loop(0, tiles, grad_products, 0)
    tail_ref[0:2, :] = gqf_ref[:16, :].astype(F32)[:2]
    tail_ref[2:4, :] = gp_ref[:16, :].astype(F32)[:2]
    tail = halo(2, seq - 1, tail_ref, head_ref)
    tail.start()
    before_ref[0:6, :] = jnp.where(here > 0, hrecv_ref[0, 0:6, :], 0.0)
    after_ref[4:8, :] = hrecv_ref[1, 2:6, :]
    tail.wait()
    after_ref[0:4, :] = jnp.where(here < seq - 1, head_ref[...], 0.0)


def last_kernel(
    k_ref, v_ref, taps_ref, mixer_ref, gqf_ref, gp_ref, before_ref, after_ref,
    out_ref, gq_ref, gk_ref, gv_ref,
):
    count = k_ref.shape[0]
    gp = gp_ref[...].astype(F32)
    gqf_next = after_ref[0:2]
    gp_next = after_ref[2:4]

    def both(ref, m):
        x = ref[...].astype(F32)
        taps = taps_ref[3 * m : 3 * m + 3]
        new = after_ref[2 + 2 * m : 4 + 2 * m]
        near, far = x[count - 1 : count], x[count - 2 : count - 1]
        first = new[0:1] * taps[0:1] + near * taps[1:2] + far * taps[2:3]
        second = new[1:2] * taps[0:1] + new[0:1] * taps[1:2] + near * taps[2:3]
        inside = causal(x, before_ref[2 * m : 2 * m + 2], taps)
        return inside, jnp.concatenate([first, second], axis=0)

    kf, kf_next = both(k_ref, 1)
    vf, vf_next = both(v_ref, 2)
    out_ref[...] = mixer_ref[...]
    gq_ref[...] = anticausal(gqf_ref[...].astype(F32), gqf_next, taps_ref[0:3]).astype(BF16)
    gk_ref[...] = anticausal(
        rounded(gp * vf), rounded(gp_next * vf_next), taps_ref[3:6]
    ).astype(BF16)
    gv_ref[...] = anticausal(
        rounded(gp * kf), rounded(gp_next * kf_next), taps_ref[6:9]
    ).astype(BF16)


def local(query_proj, key_proj, value_proj, short_filter, long_filter, out_weight, grad_out):
    count, width = query_proj.shape
    seq = lax.axis_size("seq")
    chan = lax.axis_size("chan")
    per = width // seq
    gw = min(per, GROUP)
    groups = per // gw
    length = long_filter.shape[1]
    depth, columns = out_weight.shape

    taps = jnp.repeat(short_filter.transpose(0, 2, 1).reshape(9, -1), GROUP, axis=1)
    first = lax.axis_index("seq") * per // GROUP
    chosen = lax.dynamic_slice_in_dim(long_filter, first, groups, 0).astype(F32)

    vmem = pl.BlockSpec(memory_space=pltpu.VMEM)
    flat = jax.ShapeDtypeStruct((count, width), BF16)
    rims = jax.ShapeDtypeStruct((8, width), F32)
    mixer_out, grad_qf, grad_prod, before, after = pl.pallas_call(
        step_kernel,
        in_specs=[vmem] * 5 + [pl.BlockSpec(memory_space=pl.ANY), vmem],
        out_specs=[vmem] * 5,
        out_shape=[jax.ShapeDtypeStruct((count, columns), BF16), flat, flat, rims, rims],
        scratch_shapes=[
            pltpu.VMEM((depth, columns), BF16),
            pltpu.VMEM((columns, count), BF16),
            pltpu.VMEM((groups, length), F32),
            pltpu.VMEM((groups, length, count), BF16),
            pltpu.VMEM((4, seq, groups, gw, count), BF16),
            pltpu.VMEM((4, seq, groups, gw, count), BF16),
            pltpu.VMEM((chan - 1, width, count), BF16),
            pltpu.VMEM((chan, width, count), BF16),
            pltpu.VMEM((chan, count, width), BF16),
            pltpu.VMEM((count, columns), F32),
            pltpu.VMEM((2, 8, width), F32),
            pltpu.VMEM((2, 8, width), F32),
            pltpu.VMEM((4, width), F32),
            pltpu.VMEM((4, width), F32),
            pltpu.SemaphoreType.DMA((chan,)),
            pltpu.SemaphoreType.DMA((4, seq)),
            pltpu.SemaphoreType.DMA((4, seq)),
            pltpu.SemaphoreType.DMA((2, chan)),
            pltpu.SemaphoreType.DMA((2, chan)),
            pltpu.SemaphoreType.DMA((3,)),
            pltpu.SemaphoreType.DMA((3,)),
        ],
        compiler_params=pltpu.CompilerParams(
            collective_id=0, has_side_effects=True, vmem_limit_bytes=62 * 1024 * 1024
        ),
        name="step",
    )(query_proj, key_proj, value_proj, taps, chosen, out_weight, grad_out)

    tile = min(512, width)

    def tall(rows):
        return pl.BlockSpec((rows, tile), lambda i: (0, i))

    return pl.pallas_call(
        last_kernel,
        grid=(width // tile,),
        in_specs=[tall(count), tall(count), tall(9)] + [tall(count)] * 3 + [tall(8)] * 2,
        out_specs=[tall(count)] * 4,
        out_shape=[flat] * 4,
        compiler_params=pltpu.CompilerParams(vmem_limit_bytes=32 * 1024 * 1024),
        name="last",
    )(key_proj, value_proj, taps, mixer_out, grad_qf, grad_prod, before, after)


def solution(mesh):
    return jax.shard_map(
        local,
        mesh=mesh,
        in_specs=(
            P("seq", "chan"),
            P("seq", "chan"),
            P("seq", "chan"),
            P(None, "chan", None),
            P("chan", None),
            P(None, "chan"),
            P("seq", "chan"),
        ),
        out_specs=(P("seq", "chan"), P("seq", "chan"), P("seq", "chan"), P("seq", "chan")),
        check_vma=False,
    )
```

```python
import jax
import jax.numpy as jnp
from jax import lax
from jax.experimental import pallas as pl
from jax.experimental.pallas import tpu as pltpu
from jax.sharding import PartitionSpec as P

GROUP = 16
F32 = jnp.float32
BF16 = jnp.bfloat16
MESH = pl.DeviceIdType.MESH


def causal(x, before, taps):
    row = lax.broadcasted_iota(jnp.int32, x.shape, 0)
    one = jnp.where(row == 0, before[1:2], pltpu.roll(x, 1, 0))
    two = jnp.where(row == 0, before[0:1], jnp.where(row == 1, before[1:2], pltpu.roll(x, 2, 0)))
    return x * taps[0:1] + one * taps[1:2] + two * taps[2:3]


def anticausal(g, after, taps):
    count = g.shape[0]
    row = lax.broadcasted_iota(jnp.int32, g.shape, 0)
    one = jnp.where(row == count - 1, after[0:1], pltpu.roll(g, count - 1, 0))
    two = jnp.where(
        row == count - 1,
        after[1:2],
        jnp.where(row == count - 2, after[0:1], pltpu.roll(g, count - 2, 0)),
    )
    return g * taps[0:1] + one * taps[1:2] + two * taps[2:3]


def rounded(x):
    return x.astype(BF16).astype(F32)


def step_kernel(
    q_ref, k_ref, v_ref, taps_ref, h_ref, w_hbm, go_ref,
    out_ref, gqf_ref, gp_ref, before_ref, after_ref,
    w_ref, got_ref, hr_ref, filt_ref, send_refs, recv_refs, part_send, part_recv, gall_ref,
    acc_ref, hsend_ref, hrecv_ref, tail_ref, head_ref,
    w_sem, seq_send, seq_recv, chan_send, chan_recv, halo_send, halo_recv,
):
    seq = lax.axis_size("seq")
    chan = lax.axis_size("chan")
    here = lax.axis_index("seq")
    mine = lax.axis_index("chan")
    count, width = q_ref.shape
    _, groups, gw, _ = recv_refs.shape[1:]
    per = groups * gw
    length = h_ref.shape[1]
    columns = go_ref.shape[1]
    tile = max(per, min(256, width))
    tiles = width // tile
    dests = tile // per
    rows = min(512, width)
    wide = min(512, columns)

    def seq_peer(off):
        return lax.rem(here + off, seq)

    def chan_peer(off):
        return lax.rem(mine + off, chan)

    def w_copy(off):
        at = pl.ds(pl.multiple_of(chan_peer(off) * width, width), width)
        return pltpu.make_async_copy(w_hbm.at[at], w_ref.at[at], w_sem.at[off])

    order = [off % chan for off in range(1, chan + 1)]
    for off in order:
        w_copy(off).start()

    barrier = pltpu.get_barrier_semaphore()

    def greet_seq(off, carry):
        pl.semaphore_signal(
            barrier, inc=1, device_id={"seq": seq_peer(off)}, device_id_type=MESH
        )
        return carry

    def greet_chan(off, carry):
        pl.semaphore_signal(
            barrier, inc=1, device_id={"chan": chan_peer(off)}, device_id_type=MESH
        )
        return carry

    lax.fori_loop(1, seq, greet_seq, 0)
    lax.fori_loop(1, chan, greet_chan, 0)

    for m, ref in enumerate((q_ref, k_ref, v_ref)):
        hsend_ref[0, 2 * m : 2 * m + 2, :] = ref[count - 16 :, :].astype(F32)[14:]
        hsend_ref[1, 2 * m : 2 * m + 2, :] = ref[:16, :].astype(F32)[:2]
    pl.semaphore_wait(barrier, seq + chan - 2)

    def halo(slot, by, src, dst):
        return pltpu.make_async_remote_copy(
            src_ref=src, dst_ref=dst, send_sem=halo_send.at[slot], recv_sem=halo_recv.at[slot],
            device_id={"seq": seq_peer(by)}, device_id_type=MESH,
        )

    halo_down = halo(0, 1, hsend_ref.at[0, 0:6], hrecv_ref.at[0, 0:6])
    halo_up = halo(1, seq - 1, hsend_ref.at[1, 0:6], hrecv_ref.at[1, 0:6])
    halo_down.start()
    halo_up.start()

    def turn(i, carry):
        at = pl.ds(pl.multiple_of(i * wide, wide), wide)
        got_ref[at, :] = go_ref[:, at].astype(F32).T.astype(BF16)
        return carry

    lax.fori_loop(0, columns // wide, turn, 0)

    def exchange(slot, off):
        return pltpu.make_async_remote_copy(
            src_ref=send_refs.at[slot, seq_peer(off)],
            dst_ref=recv_refs.at[slot, here],
            send_sem=seq_send.at[slot, off],
            recv_sem=seq_recv.at[slot, off],
            device_id={"seq": seq_peer(off)},
            device_id_type=MESH,
        )

    def exchange_start(slot):
        def go(off, carry):
            exchange(slot, off).start()
            return carry

        lax.fori_loop(1, seq, go, 0)
        recv_refs[slot, pl.ds(here, 1)] = send_refs[slot, pl.ds(here, 1)]

    def exchange_wait(slot):
        def go(off, carry):
            exchange(slot, off).wait()
            return carry

        lax.fori_loop(1, seq, go, 0)

    def to_send(slot, i, turned):
        send_refs[slot, pl.ds(i * dests, dests)] = turned.reshape(
            dests, groups, gw, count
        ).astype(BF16)

    def from_recv(slot, i):
        return recv_refs[slot, pl.ds(i * dests, dests)].astype(F32).reshape(tile, count)

    def cols(i):
        return pl.ds(pl.multiple_of(i * tile, tile), tile)

    def filtered(ref, m, at):
        ahead = jnp.where(here > 0, hrecv_ref[0, 2 * m : 2 * m + 2, at], 0.0)
        return causal(ref[:, at].astype(F32), ahead, taps_ref[3 * m : 3 * m + 3, at])

    halo_down.wait()
    halo_up.wait()

    def spread(slot, make):
        def one(i, carry):
            to_send(slot, i, make(cols(i)))
            return carry

        def off_to(off, carry):
            one(seq_peer(off), 0)
            exchange(slot, off).start()
            return carry

        if dests == 1:
            lax.fori_loop(1, seq, off_to, 0)
            one(here, 0)
            recv_refs[slot, pl.ds(here, 1)] = send_refs[slot, pl.ds(here, 1)]
        else:
            lax.fori_loop(0, tiles, one, 0)
            exchange_start(slot)

    spread(0, lambda at: (filtered(k_ref, 1, at) * filtered(v_ref, 2, at)).T)

    def part(off):
        return pltpu.make_async_remote_copy(
            src_ref=part_send.at[off - 1],
            dst_ref=part_recv.at[mine],
            send_sem=chan_send.at[0, off],
            recv_sem=chan_recv.at[0, off],
            device_id={"chan": chan_peer(off)},
            device_id_type=MESH,
        )

    def back_project(off):
        w_copy(off).wait()

        def some(i, carry):
            start = pl.multiple_of(chan_peer(off) * width + i * rows, rows)
            got = jnp.dot(w_ref[pl.ds(start, rows), :], got_ref[...], preferred_element_type=F32)
            at = pl.ds(pl.multiple_of(i * rows, rows), rows)
            if off:
                part_send[off - 1, at, :] = got.astype(BF16)
            else:
                part_recv[mine, at, :] = got.astype(BF16)
            return carry

        lax.fori_loop(0, width // rows, some, 0)
        if off:
            part(off).start()

    for off in range(1, chan):
        back_project(off)

    flip = (
        lax.broadcasted_iota(jnp.int32, (count, count), 0)
        + lax.broadcasted_iota(jnp.int32, (count, count), 1)
        == count - 1
    )
    flip = jnp.where(flip, 1.0, 0.0).astype(BF16)
    for k in range(length // count):
        hr_ref[:, length - (k + 1) * count : length - k * count] = jnp.dot(
            h_ref[:, k * count : (k + 1) * count].astype(BF16), flip, preferred_element_type=F32
        )

    def build(forward):
        def one(g, carry):
            pad = jnp.zeros((count, count), F32)
            row = (h_ref if forward else hr_ref)[pl.ds(g, 1), :]
            lines = jnp.broadcast_to(row, (count, length))
            pair = [pad, lines] if forward else [lines, pad]
            lined = pltpu.roll(
                jnp.concatenate(pair, axis=1), 0 if forward else 1, 1, stride=1, stride_axis=0
            ).astype(BF16)
            for k in range(length // count):
                at = (k + 1) * count if forward else length - k * count
                filt_ref[g, k * count : (k + 1) * count, :] = lined[:, at : at + count]
            return carry

        lax.fori_loop(0, groups, one, 0)

    def mix(forward, slot):
        total_rows = seq * gw

        def one(g, carry):
            x = recv_refs[slot, :, g]
            kind = F32 if gw % 16 else BF16
            x = x.astype(kind).reshape(total_rows, count)
            pieces = [x.astype(BF16)]
            for k in range(1, seq):
                pad = jnp.zeros((k * gw, count), kind)
                if forward:
                    moved = jnp.concatenate([pad, x[: total_rows - k * gw]], axis=0)
                else:
                    moved = jnp.concatenate([x[k * gw :], pad], axis=0)
                pieces.append(moved.astype(BF16))
            total = jnp.dot(
                jnp.concatenate(pieces, axis=1), filt_ref[g], preferred_element_type=F32
            )
            send_refs[slot + 1, :, g] = total.reshape(seq, gw, count).astype(BF16)
            return carry

        lax.fori_loop(0, groups, one, 0)

    build(True)
    exchange_wait(0)
    mix(True, 0)
    exchange_start(1)
    back_project(0)
    build(False)

    for off in range(1, chan):
        part(off).wait()

    def summed(at):
        return jnp.sum(part_recv[:, at, :].astype(F32), axis=0)

    spread(2, lambda at: summed(at) * filtered(q_ref, 0, at).T)

    def share(off):
        return pltpu.make_async_remote_copy(
            src_ref=gall_ref.at[mine],
            dst_ref=gall_ref.at[mine],
            send_sem=chan_send.at[1, off],
            recv_sem=chan_recv.at[1, off],
            device_id={"chan": chan_peer(off)},
            device_id_type=MESH,
        )

    exchange_wait(1)

    def gate(i, carry):
        at = cols(i)
        gall_ref[mine, :, at] = (filtered(q_ref, 0, at) * from_recv(1, i).T).astype(BF16)
        return carry

    lax.fori_loop(0, tiles, gate, 0)
    for off in range(1, chan):
        share(off).start()

    def grad_query(i, carry):
        at = cols(i)
        gqf_ref[:, at] = (summed(at) * from_recv(1, i)).T.astype(BF16)
        return carry

    lax.fori_loop(0, tiles, grad_query, 0)

    def project(off, first, last):
        owner = chan_peer(chan - off)

        def some(i, carry):
            at = pl.ds(pl.multiple_of(i * wide, wide), wide)
            start = pl.multiple_of(owner * width, width)
            got = jnp.dot(
                gall_ref[owner], w_ref[pl.ds(start, width), at], preferred_element_type=F32
            )
            if not first:
                got = got + acc_ref[:, at]
            if last:
                out_ref[:, at] = got.astype(BF16)
            else:
                acc_ref[:, at] = got
            return carry

        lax.fori_loop(0, columns // wide, some, 0)

    project(0, True, chan == 1)
    exchange_wait(2)
    mix(False, 2)
    exchange_start(3)
    for off in range(1, chan):
        share(off).wait()
        project(off, False, off == chan - 1)

    exchange_wait(3)

    def grad_products(i, carry):
        at = cols(i)
        gp_ref[:, at] = from_recv(3, i).T.astype(BF16)
        return carry

    lax.fori_loop(0, tiles, grad_products, 0)
    tail_ref[0:2, :] = gqf_ref[:16, :].astype(F32)[:2]
    tail_ref[2:4, :] = gp_ref[:16, :].astype(F32)[:2]
    tail = halo(2, seq - 1, tail_ref, head_ref)
    tail.start()
    before_ref[0:6, :] = jnp.where(here > 0, hrecv_ref[0, 0:6, :], 0.0)
    after_ref[4:8, :] = hrecv_ref[1, 2:6, :]
    tail.wait()
    after_ref[0:4, :] = jnp.where(here < seq - 1, head_ref[...], 0.0)


def last_kernel(
    k_ref, v_ref, taps_ref, mixer_ref, gqf_ref, gp_ref, before_ref, after_ref,
    out_ref, gq_ref, gk_ref, gv_ref,
):
    count = k_ref.shape[0]
    gp = gp_ref[...].astype(F32)
    gqf_next = after_ref[0:2]
    gp_next = after_ref[2:4]

    def both(ref, m):
        x = ref[...].astype(F32)
        taps = taps_ref[3 * m : 3 * m + 3]
        new = after_ref[2 + 2 * m : 4 + 2 * m]
        near, far = x[count - 1 : count], x[count - 2 : count - 1]
        first = new[0:1] * taps[0:1] + near * taps[1:2] + far * taps[2:3]
        second = new[1:2] * taps[0:1] + new[0:1] * taps[1:2] + near * taps[2:3]
        inside = causal(x, before_ref[2 * m : 2 * m + 2], taps)
        return inside, jnp.concatenate([first, second], axis=0)

    kf, kf_next = both(k_ref, 1)
    vf, vf_next = both(v_ref, 2)
    out_ref[...] = mixer_ref[...]
    gq_ref[...] = anticausal(gqf_ref[...].astype(F32), gqf_next, taps_ref[0:3]).astype(BF16)
    gk_ref[...] = anticausal(
        rounded(gp * vf), rounded(gp_next * vf_next), taps_ref[3:6]
    ).astype(BF16)
    gv_ref[...] = anticausal(
        rounded(gp * kf), rounded(gp_next * kf_next), taps_ref[6:9]
    ).astype(BF16)


def local(query_proj, key_proj, value_proj, short_filter, long_filter, out_weight, grad_out):
    count, width = query_proj.shape
    seq = lax.axis_size("seq")
    chan = lax.axis_size("chan")
    per = width // seq
    gw = min(per, GROUP)
    groups = per // gw
    length = long_filter.shape[1]
    depth, columns = out_weight.shape

    taps = jnp.repeat(short_filter.transpose(0, 2, 1).reshape(9, -1), GROUP, axis=1)
    first = lax.axis_index("seq") * per // GROUP
    chosen = lax.dynamic_slice_in_dim(long_filter, first, groups, 0).astype(F32)

    vmem = pl.BlockSpec(memory_space=pltpu.VMEM)
    flat = jax.ShapeDtypeStruct((count, width), BF16)
    rims = jax.ShapeDtypeStruct((8, width), F32)
    mixer_out, grad_qf, grad_prod, before, after = pl.pallas_call(
        step_kernel,
        in_specs=[vmem] * 5 + [pl.BlockSpec(memory_space=pl.ANY), vmem],
        out_specs=[vmem] * 5,
        out_shape=[jax.ShapeDtypeStruct((count, columns), BF16), flat, flat, rims, rims],
        scratch_shapes=[
            pltpu.VMEM((depth, columns), BF16),
            pltpu.VMEM((columns, count), BF16),
            pltpu.VMEM((groups, length), F32),
            pltpu.VMEM((groups, length, count), BF16),
            pltpu.VMEM((4, seq, groups, gw, count), BF16),
            pltpu.VMEM((4, seq, groups, gw, count), BF16),
            pltpu.VMEM((chan - 1, width, count), BF16),
            pltpu.VMEM((chan, width, count), BF16),
            pltpu.VMEM((chan, count, width), BF16),
            pltpu.VMEM((count, columns), F32),
            pltpu.VMEM((2, 8, width), F32),
            pltpu.VMEM((2, 8, width), F32),
            pltpu.VMEM((4, width), F32),
            pltpu.VMEM((4, width), F32),
            pltpu.SemaphoreType.DMA((chan,)),
            pltpu.SemaphoreType.DMA((4, seq)),
            pltpu.SemaphoreType.DMA((4, seq)),
            pltpu.SemaphoreType.DMA((2, chan)),
            pltpu.SemaphoreType.DMA((2, chan)),
            pltpu.SemaphoreType.DMA((3,)),
            pltpu.SemaphoreType.DMA((3,)),
        ],
        compiler_params=pltpu.CompilerParams(
            collective_id=0, has_side_effects=True, vmem_limit_bytes=62 * 1024 * 1024
        ),
        name="step",
    )(query_proj, key_proj, value_proj, taps, chosen, out_weight, grad_out)

    tile = min(512, width)

    def tall(rows):
        return pl.BlockSpec((rows, tile), lambda i: (0, i))

    return pl.pallas_call(
        last_kernel,
        grid=(width // tile,),
        in_specs=[tall(count), tall(count), tall(9)] + [tall(count)] * 3 + [tall(8)] * 2,
        out_specs=[tall(count)] * 4,
        out_shape=[flat] * 4,
        compiler_params=pltpu.CompilerParams(vmem_limit_bytes=62 * 1024 * 1024),
        name="last",
    )(key_proj, value_proj, taps, mixer_out, grad_qf, grad_prod, before, after)


def solution(mesh):
    return jax.shard_map(
        local,
        mesh=mesh,
        in_specs=(
            P("seq", "chan"),
            P("seq", "chan"),
            P("seq", "chan"),
            P(None, "chan", None),
            P("chan", None),
            P(None, "chan"),
            P("seq", "chan"),
        ),
        out_specs=(P("seq", "chan"), P("seq", "chan"), P("seq", "chan"), P("seq", "chan")),
        check_vma=False,
    )
```

```python
import jax
import jax.numpy as jnp
from jax import lax
from jax.experimental import pallas as pl
from jax.experimental.pallas import tpu as pltpu
from jax.sharding import PartitionSpec as P

GROUP = 16
F32 = jnp.float32
BF16 = jnp.bfloat16
MESH = pl.DeviceIdType.MESH


def causal(x, before, taps):
    row = lax.broadcasted_iota(jnp.int32, x.shape, 0)
    one = jnp.where(row == 0, before[1:2], pltpu.roll(x, 1, 0))
    two = jnp.where(row == 0, before[0:1], jnp.where(row == 1, before[1:2], pltpu.roll(x, 2, 0)))
    return x * taps[0:1] + one * taps[1:2] + two * taps[2:3]


def anticausal(g, after, taps):
    count = g.shape[0]
    row = lax.broadcasted_iota(jnp.int32, g.shape, 0)
    one = jnp.where(row == count - 1, after[0:1], pltpu.roll(g, count - 1, 0))
    two = jnp.where(
        row == count - 1,
        after[1:2],
        jnp.where(row == count - 2, after[0:1], pltpu.roll(g, count - 2, 0)),
    )
    return g * taps[0:1] + one * taps[1:2] + two * taps[2:3]


def rounded(x):
    return x.astype(BF16).astype(F32)


def step_kernel(
    q_ref, k_ref, v_ref, taps_ref, h_ref, w_hbm, go_ref,
    out_ref, gqf_ref, gp_ref, before_ref, after_ref,
    w_ref, got_ref, hr_ref, filt_ref, send_refs, recv_refs, part_send, part_recv, gall_ref,
    acc_ref, hsend_ref, hrecv_ref, tail_ref, head_ref,
    w_sem, seq_send, seq_recv, chan_send, chan_recv, halo_send, halo_recv,
):
    seq = lax.axis_size("seq")
    chan = lax.axis_size("chan")
    here = lax.axis_index("seq")
    mine = lax.axis_index("chan")
    count, width = q_ref.shape
    _, groups, gw, _ = recv_refs.shape[1:]
    per = groups * gw
    length = h_ref.shape[1]
    columns = go_ref.shape[1]
    tile = max(per, min(256, width))
    tiles = width // tile
    dests = tile // per
    rows = min(512, width)
    wide = min(512, columns)

    def seq_peer(off):
        return lax.rem(here + off, seq)

    def chan_peer(off):
        return lax.rem(mine + off, chan)

    def w_copy(off):
        at = pl.ds(pl.multiple_of(chan_peer(off) * width, width), width)
        return pltpu.make_async_copy(w_hbm.at[at], w_ref.at[at], w_sem.at[off])

    order = [off % chan for off in range(1, chan + 1)]
    for off in order:
        w_copy(off).start()

    barrier = pltpu.get_barrier_semaphore()

    def greet_seq(off, carry):
        pl.semaphore_signal(
            barrier, inc=1, device_id={"seq": seq_peer(off)}, device_id_type=MESH
        )
        return carry

    def greet_chan(off, carry):
        pl.semaphore_signal(
            barrier, inc=1, device_id={"chan": chan_peer(off)}, device_id_type=MESH
        )
        return carry

    lax.fori_loop(1, seq, greet_seq, 0)
    lax.fori_loop(1, chan, greet_chan, 0)

    for m, ref in enumerate((q_ref, k_ref, v_ref)):
        hsend_ref[0, 2 * m : 2 * m + 2, :] = ref[count - 16 :, :].astype(F32)[14:]
        hsend_ref[1, 2 * m : 2 * m + 2, :] = ref[:16, :].astype(F32)[:2]
    pl.semaphore_wait(barrier, seq + chan - 2)

    def halo(slot, by, src, dst):
        return pltpu.make_async_remote_copy(
            src_ref=src, dst_ref=dst, send_sem=halo_send.at[slot], recv_sem=halo_recv.at[slot],
            device_id={"seq": seq_peer(by)}, device_id_type=MESH,
        )

    halo_down = halo(0, 1, hsend_ref.at[0, 0:6], hrecv_ref.at[0, 0:6])
    halo_up = halo(1, seq - 1, hsend_ref.at[1, 0:6], hrecv_ref.at[1, 0:6])
    halo_down.start()
    halo_up.start()

    def turn(i, carry):
        at = pl.ds(pl.multiple_of(i * wide, wide), wide)
        got_ref[at, :] = go_ref[:, at].astype(F32).T.astype(BF16)
        return carry

    lax.fori_loop(0, columns // wide, turn, 0)

    def exchange(slot, off):
        return pltpu.make_async_remote_copy(
            src_ref=send_refs.at[slot, seq_peer(off)],
            dst_ref=recv_refs.at[slot, here],
            send_sem=seq_send.at[slot, off],
            recv_sem=seq_recv.at[slot, off],
            device_id={"seq": seq_peer(off)},
            device_id_type=MESH,
        )

    def exchange_start(slot):
        def go(off, carry):
            exchange(slot, off).start()
            return carry

        lax.fori_loop(1, seq, go, 0)
        recv_refs[slot, pl.ds(here, 1)] = send_refs[slot, pl.ds(here, 1)]

    def exchange_wait(slot):
        def go(off, carry):
            exchange(slot, off).wait()
            return carry

        lax.fori_loop(1, seq, go, 0)

    def to_send(slot, i, turned):
        send_refs[slot, pl.ds(i * dests, dests)] = turned.reshape(
            dests, groups, gw, count
        ).astype(BF16)

    def from_recv(slot, i):
        return recv_refs[slot, pl.ds(i * dests, dests)].astype(F32).reshape(tile, count)

    def cols(i):
        return pl.ds(pl.multiple_of(i * tile, tile), tile)

    def filtered(ref, m, at):
        ahead = jnp.where(here > 0, hrecv_ref[0, 2 * m : 2 * m + 2, at], 0.0)
        return causal(ref[:, at].astype(F32), ahead, taps_ref[3 * m : 3 * m + 3, at])

    flip = (
        lax.broadcasted_iota(jnp.int32, (count, count), 0)
        + lax.broadcasted_iota(jnp.int32, (count, count), 1)
        == count - 1
    )
    flip = jnp.where(flip, 1.0, 0.0).astype(BF16)
    for k in range(length // count):
        hr_ref[:, length - (k + 1) * count : length - k * count] = jnp.dot(
            h_ref[:, k * count : (k + 1) * count].astype(BF16), flip, preferred_element_type=F32
        )

    def build(forward):
        def one(g, carry):
            pad = jnp.zeros((count, count), F32)
            row = (h_ref if forward else hr_ref)[pl.ds(g, 1), :]
            lines = jnp.broadcast_to(row, (count, length))
            pair = [pad, lines] if forward else [lines, pad]
            lined = pltpu.roll(
                jnp.concatenate(pair, axis=1), 0 if forward else 1, 1, stride=1, stride_axis=0
            ).astype(BF16)
            for k in range(length // count):
                at = (k + 1) * count if forward else length - k * count
                filt_ref[g, k * count : (k + 1) * count, :] = lined[:, at : at + count]
            return carry

        lax.fori_loop(0, groups, one, 0)

    build(True)
    halo_down.wait()
    halo_up.wait()

    def spread(slot, make):
        def one(i, carry):
            to_send(slot, i, make(cols(i)))
            return carry

        def off_to(off, carry):
            one(seq_peer(off), 0)
            exchange(slot, off).start()
            return carry

        if dests == 1:
            lax.fori_loop(1, seq, off_to, 0)
            one(here, 0)
            recv_refs[slot, pl.ds(here, 1)] = send_refs[slot, pl.ds(here, 1)]
        else:
            lax.fori_loop(0, tiles, one, 0)
            exchange_start(slot)

    spread(0, lambda at: (filtered(k_ref, 1, at) * filtered(v_ref, 2, at)).T)

    def part(off):
        return pltpu.make_async_remote_copy(
            src_ref=part_send.at[off - 1],
            dst_ref=part_recv.at[mine],
            send_sem=chan_send.at[0, off],
            recv_sem=chan_recv.at[0, off],
            device_id={"chan": chan_peer(off)},
            device_id_type=MESH,
        )

    def back_project(off):
        w_copy(off).wait()

        def some(i, carry):
            start = pl.multiple_of(chan_peer(off) * width + i * rows, rows)
            got = jnp.dot(w_ref[pl.ds(start, rows), :], got_ref[...], preferred_element_type=F32)
            at = pl.ds(pl.multiple_of(i * rows, rows), rows)
            if off:
                part_send[off - 1, at, :] = got.astype(BF16)
            else:
                part_recv[mine, at, :] = got.astype(BF16)
            return carry

        lax.fori_loop(0, width // rows, some, 0)
        if off:
            part(off).start()

    for off in range(1, chan):
        back_project(off)

    def mix(forward, slot):
        total_rows = seq * gw

        def one(g, carry):
            x = recv_refs[slot, :, g]
            kind = F32 if gw % 16 else BF16
            x = x.astype(kind).reshape(total_rows, count)
            pieces = [x.astype(BF16)]
            for k in range(1, seq):
                pad = jnp.zeros((k * gw, count), kind)
                if forward:
                    moved = jnp.concatenate([pad, x[: total_rows - k * gw]], axis=0)
                else:
                    moved = jnp.concatenate([x[k * gw :], pad], axis=0)
                pieces.append(moved.astype(BF16))
            total = jnp.dot(
                jnp.concatenate(pieces, axis=1), filt_ref[g], preferred_element_type=F32
            )
            send_refs[slot + 1, :, g] = total.reshape(seq, gw, count).astype(BF16)
            return carry

        lax.fori_loop(0, groups, one, 0)

    exchange_wait(0)
    mix(True, 0)
    exchange_start(1)
    back_project(0)
    build(False)

    for off in range(1, chan):
        part(off).wait()

    def summed(at):
        return jnp.sum(part_recv[:, at, :].astype(F32), axis=0)

    spread(2, lambda at: summed(at) * filtered(q_ref, 0, at).T)

    def share(off):
        return pltpu.make_async_remote_copy(
            src_ref=gall_ref.at[mine],
            dst_ref=gall_ref.at[mine],
            send_sem=chan_send.at[1, off],
            recv_sem=chan_recv.at[1, off],
            device_id={"chan": chan_peer(off)},
            device_id_type=MESH,
        )

    exchange_wait(1)

    def gate(i, carry):
        at = cols(i)
        gall_ref[mine, :, at] = (filtered(q_ref, 0, at) * from_recv(1, i).T).astype(BF16)
        return carry

    lax.fori_loop(0, tiles, gate, 0)
    for off in range(1, chan):
        share(off).start()

    def grad_query(i, carry):
        at = cols(i)
        gqf_ref[:, at] = (summed(at) * from_recv(1, i)).T.astype(BF16)
        return carry

    lax.fori_loop(0, tiles, grad_query, 0)

    def project(off, first, last):
        owner = chan_peer(chan - off)

        def some(i, carry):
            at = pl.ds(pl.multiple_of(i * wide, wide), wide)
            start = pl.multiple_of(owner * width, width)
            got = jnp.dot(
                gall_ref[owner], w_ref[pl.ds(start, width), at], preferred_element_type=F32
            )
            if not first:
                got = got + acc_ref[:, at]
            if last:
                out_ref[:, at] = got.astype(BF16)
            else:
                acc_ref[:, at] = got
            return carry

        lax.fori_loop(0, columns // wide, some, 0)

    project(0, True, chan == 1)
    exchange_wait(2)
    mix(False, 2)
    exchange_start(3)
    for off in range(1, chan):
        share(off).wait()
        project(off, False, off == chan - 1)

    exchange_wait(3)

    def grad_products(i, carry):
        at = cols(i)
        gp_ref[:, at] = from_recv(3, i).T.astype(BF16)
        return carry

    lax.fori_loop(0, tiles, grad_products, 0)
    tail_ref[0:2, :] = gqf_ref[:16, :].astype(F32)[:2]
    tail_ref[2:4, :] = gp_ref[:16, :].astype(F32)[:2]
    tail = halo(2, seq - 1, tail_ref, head_ref)
    tail.start()
    before_ref[0:6, :] = jnp.where(here > 0, hrecv_ref[0, 0:6, :], 0.0)
    after_ref[4:8, :] = hrecv_ref[1, 2:6, :]
    tail.wait()
    after_ref[0:4, :] = jnp.where(here < seq - 1, head_ref[...], 0.0)


def last_kernel(
    k_ref, v_ref, taps_ref, mixer_ref, gqf_ref, gp_ref, before_ref, after_ref,
    out_ref, gq_ref, gk_ref, gv_ref,
):
    count = k_ref.shape[0]
    gp = gp_ref[...].astype(F32)
    gqf_next = after_ref[0:2]
    gp_next = after_ref[2:4]

    def both(ref, m):
        x = ref[...].astype(F32)
        taps = taps_ref[3 * m : 3 * m + 3]
        new = after_ref[2 + 2 * m : 4 + 2 * m]
        near, far = x[count - 1 : count], x[count - 2 : count - 1]
        first = new[0:1] * taps[0:1] + near * taps[1:2] + far * taps[2:3]
        second = new[1:2] * taps[0:1] + new[0:1] * taps[1:2] + near * taps[2:3]
        inside = causal(x, before_ref[2 * m : 2 * m + 2], taps)
        return inside, jnp.concatenate([first, second], axis=0)

    kf, kf_next = both(k_ref, 1)
    vf, vf_next = both(v_ref, 2)
    out_ref[...] = mixer_ref[...]
    gq_ref[...] = anticausal(gqf_ref[...].astype(F32), gqf_next, taps_ref[0:3]).astype(BF16)
    gk_ref[...] = anticausal(
        rounded(gp * vf), rounded(gp_next * vf_next), taps_ref[3:6]
    ).astype(BF16)
    gv_ref[...] = anticausal(
        rounded(gp * kf), rounded(gp_next * kf_next), taps_ref[6:9]
    ).astype(BF16)


def local(query_proj, key_proj, value_proj, short_filter, long_filter, out_weight, grad_out):
    count, width = query_proj.shape
    seq = lax.axis_size("seq")
    chan = lax.axis_size("chan")
    per = width // seq
    gw = min(per, GROUP)
    groups = per // gw
    length = long_filter.shape[1]
    depth, columns = out_weight.shape

    taps = jnp.repeat(short_filter.transpose(0, 2, 1).reshape(9, -1), GROUP, axis=1)
    first = lax.axis_index("seq") * per // GROUP
    chosen = lax.dynamic_slice_in_dim(long_filter, first, groups, 0).astype(F32)

    vmem = pl.BlockSpec(memory_space=pltpu.VMEM)
    flat = jax.ShapeDtypeStruct((count, width), BF16)
    rims = jax.ShapeDtypeStruct((8, width), F32)
    mixer_out, grad_qf, grad_prod, before, after = pl.pallas_call(
        step_kernel,
        in_specs=[vmem] * 5 + [pl.BlockSpec(memory_space=pl.ANY), vmem],
        out_specs=[vmem] * 5,
        out_shape=[jax.ShapeDtypeStruct((count, columns), BF16), flat, flat, rims, rims],
        scratch_shapes=[
            pltpu.VMEM((depth, columns), BF16),
            pltpu.VMEM((columns, count), BF16),
            pltpu.VMEM((groups, length), F32),
            pltpu.VMEM((groups, length, count), BF16),
            pltpu.VMEM((4, seq, groups, gw, count), BF16),
            pltpu.VMEM((4, seq, groups, gw, count), BF16),
            pltpu.VMEM((chan - 1, width, count), BF16),
            pltpu.VMEM((chan, width, count), BF16),
            pltpu.VMEM((chan, count, width), BF16),
            pltpu.VMEM((count, columns), F32),
            pltpu.VMEM((2, 8, width), F32),
            pltpu.VMEM((2, 8, width), F32),
            pltpu.VMEM((4, width), F32),
            pltpu.VMEM((4, width), F32),
            pltpu.SemaphoreType.DMA((chan,)),
            pltpu.SemaphoreType.DMA((4, seq)),
            pltpu.SemaphoreType.DMA((4, seq)),
            pltpu.SemaphoreType.DMA((2, chan)),
            pltpu.SemaphoreType.DMA((2, chan)),
            pltpu.SemaphoreType.DMA((3,)),
            pltpu.SemaphoreType.DMA((3,)),
        ],
        compiler_params=pltpu.CompilerParams(
            collective_id=0, has_side_effects=True, vmem_limit_bytes=62 * 1024 * 1024
        ),
        name="step",
    )(query_proj, key_proj, value_proj, taps, chosen, out_weight, grad_out)

    tile = min(512, width)

    def tall(rows):
        return pl.BlockSpec((rows, tile), lambda i: (0, i))

    return pl.pallas_call(
        last_kernel,
        grid=(width // tile,),
        in_specs=[tall(count), tall(count), tall(9)] + [tall(count)] * 3 + [tall(8)] * 2,
        out_specs=[tall(count)] * 4,
        out_shape=[flat] * 4,
        compiler_params=pltpu.CompilerParams(vmem_limit_bytes=62 * 1024 * 1024),
        name="last",
    )(key_proj, value_proj, taps, mixer_out, grad_qf, grad_prod, before, after)


def solution(mesh):
    return jax.shard_map(
        local,
        mesh=mesh,
        in_specs=(
            P("seq", "chan"),
            P("seq", "chan"),
            P("seq", "chan"),
            P(None, "chan", None),
            P("chan", None),
            P(None, "chan"),
            P("seq", "chan"),
        ),
        out_specs=(P("seq", "chan"), P("seq", "chan"), P("seq", "chan"), P("seq", "chan")),
        check_vma=False,
    )
```
